512 devices in a mesh: tm: 64 (over z, y), tensor: 8 (over x, core).
Axes of the slice: x: 4, y: 4, z: 16, core: 2. Of those that a mesh axis runs over, the one named last changes fastest.
Arguments:
- query_input: bfloat16 [24576, 2048], P('tm', 'tensor'), may hold values from -6 to 6
- key_input: bfloat16 [24576, 2048], P('tm', 'tensor'), may hold values from -6 to 6
- value_input: bfloat16 [24576, 2048], P('tm', 'tensor'), may hold values from -6 to 6
- log_decay: float32 [16, 24576], P('tensor', 'tm'), may hold values from -0.75 to 0, as said below
- stretch_ids: int32 [24576], P('tm'), may hold values from 0 to 383, as said below
- norm_gain: float32 [2048], P('tensor'), may hold values from 0.1 to 1.9
- out_weight: bfloat16 [2048, 4096], P('tensor'), may hold values from -0.125 to 0.125
- out_cotangent: bfloat16 [24576, 4096], P(('tm', 'tensor')), may hold values from -6 to 6
Outputs:
- layer_out: bfloat16 [24576, 4096], P(('tm', 'tensor'))
- query_grad: bfloat16 [24576, 2048], P('tm', 'tensor')
- key_grad: bfloat16 [24576, 2048], P('tm', 'tensor')
- value_grad: bfloat16 [24576, 2048], P('tm', 'tensor')
The draws below stay inside these ranges and needn't reach their ends.
Inputs may be any that keep to these rules, and one draw needn't show every extreme that they name: `stretch_ids`: stretch ids never fall along the tokens, start at 0 and rise by at most one at a time, change only at multiples of 32 tokens, and rise at every multiple of 384 tokens, so that no stretch crosses a block; every block holds exactly 6 stretches. `log_decay`: every entry is negative.
All inputs are finite; a program needn't handle non-finite values.
Results may differ from the reference program's by a relative error of at most 0.014.
Values may be sent and summed in bfloat16 or wider, within the bound.
No kernel may reach another device: no remote copies, remote signals or barrier semaphores. Data moves between devices by JAX's collectives and lax.ppermute only.
A program may use at most 64 MiB of HBM per device.

```python
import math
import jax
import jax.numpy as jnp
from jax import lax

LOCAL_HEADS = 16
HD = 128
DOUT = 4096
FRAME = 32
TOK_DEV = 384
SEQUENCE_TOKENS = 24576
N_TM = 64
N_TENSOR = 8


def draw_log_decay(key, part):
    random_key_list = jax.random.split(jax.random.fold_in(key, 11), 6)
    fast_share = 0.5
    fast_head = jax.random.uniform(random_key_list[0], (LOCAL_HEADS, 1)) < fast_share
    fast_span = jnp.exp(jax.random.uniform(random_key_list[1], (LOCAL_HEADS, 1), minval=math.log(30.0), maxval=math.log(50.0)))
    slow_total = jnp.exp(jax.random.uniform(random_key_list[2], (LOCAL_HEADS, 1), minval=math.log(0.1), maxval=math.log(0.8)))
    baseline_decay_rate = jnp.where(fast_head, 1.0 / fast_span, slow_total / SEQUENCE_TOKENS)
    jagged_level = jax.random.uniform(random_key_list[3], (LOCAL_HEADS, SEQUENCE_TOKENS), minval=0.5, maxval=1.5)
    spike_positions = jax.random.randint(random_key_list[4], (LOCAL_HEADS, 2), 0, SEQUENCE_TOKENS)
    loss_values = jax.random.uniform(random_key_list[5], (LOCAL_HEADS, 2), minval=0.22, maxval=0.69)
    position_list = jnp.arange(SEQUENCE_TOKENS)[None, :]
    spike_events = jnp.where(position_list == spike_positions[:, 0:1], loss_values[:, 0:1], 0.0) + jnp.where(position_list == spike_positions[:, 1:2], loss_values[:, 1:2], 0.0)
    return (-(baseline_decay_rate * jagged_level + spike_events)).astype(jnp.float32)


def draw_stretch_ids(key, part):
    block_count = SEQUENCE_TOKENS // TOK_DEV
    frames_block = TOK_DEV // FRAME
    starts_block = max(1, frames_block // 2)
    block_keys = jax.random.split(jax.random.fold_in(key, 23), block_count)

    def block_starts(block_key):
        ranking = jax.random.permutation(block_key, jnp.arange(max(frames_block - 1, 1), dtype=jnp.int32))
        rest = (ranking[:frames_block - 1] < starts_block - 1).astype(jnp.int32)
        return jnp.concatenate([jnp.ones((1,), jnp.int32), rest])
    new_stretch = jax.vmap(block_starts)(block_keys).reshape(block_count * frames_block)
    stretch_index = jnp.cumsum(new_stretch) - 1
    return jnp.repeat(stretch_index, FRAME, total_repeat_length=SEQUENCE_TOKENS).astype(jnp.int32)


def block_scale(key, extent, cuts, low, top_value):
    def one(axis_at, shards_of):
        heights = jax.random.uniform(jax.random.fold_in(jax.random.fold_in(key, 6), axis_at), (shards_of,), jnp.float32, low / len(cuts), top_value / len(cuts))
        return jnp.repeat(jnp.exp(heights), extent[axis_at] // shards_of).reshape((-1,) + (1,) * (len(extent) - axis_at - 1))

    loudness = one(*cuts[0])
    for cut in cuts[1:]:
        loudness = loudness * one(*cut)
    return loudness


def gaussian(key, extent, deviation, limit, pieces=(), kind=jnp.bfloat16):
    gain = block_scale(key, extent, pieces, -0.22, 0.18) if pieces else 1.0
    array = jax.random.normal(key, extent, jnp.float32) * deviation * gain
    return jnp.minimum(jnp.maximum(array, -limit), limit).astype(kind)


def setup_inputs(seed: int = 0) -> dict:
    key_of = jax.random.split(jax.random.key(seed), 9)
    return {
        "query_input": gaussian(key_of[0], (SEQUENCE_TOKENS, LOCAL_HEADS * HD), 1.0, 6.0, ((0, 64), (1, 8))),
        "key_input": gaussian(key_of[1], (SEQUENCE_TOKENS, LOCAL_HEADS * HD), 1.0, 6.0, ((0, 64), (1, 8))),
        "value_input": gaussian(key_of[2], (SEQUENCE_TOKENS, LOCAL_HEADS * HD), 1.0, 6.0, ((0, 64), (1, 8))),
        "log_decay": draw_log_decay(jax.random.fold_in(key_of[8], 71), 0),
        "stretch_ids": draw_stretch_ids(jax.random.fold_in(key_of[8], 71), 0),
        "norm_gain": jnp.clip(1.0 + 0.18 * jax.random.normal(key_of[5], (LOCAL_HEADS * HD,), jnp.float32), 0.1, 1.9),
        "out_weight": gaussian(key_of[6], (LOCAL_HEADS * HD, DOUT), (LOCAL_HEADS * HD) ** -0.5, 0.125, ((0, 8),)),
        "out_cotangent": gaussian(key_of[7], (SEQUENCE_TOKENS, DOUT), 1.0, 6.0, ((0, 512),)),
    }


def local_parts(query_blk, key_blk, decay_blk, stretch_blk):
    query_pos = jnp.maximum(query_blk, 0)
    key_pos = jnp.maximum(key_blk, 0)
    cumulative = jnp.cumsum(decay_blk, axis=1)
    same_stretch = stretch_blk[:, None] == stretch_blk[None, :]
    visible = stretch_blk[None, :] <= stretch_blk[:, None]
    stretch_end = lax.optimization_barrier(jnp.min(jnp.where(same_stretch[None], cumulative[:, None, :], jnp.inf), axis=2))
    block_end = cumulative[:, -1]
    weights = jnp.where(visible[None], jnp.exp(jnp.minimum(stretch_end[:, :, None] - cumulative[:, None, :], 0.0)), 0.0)
    scores = jnp.einsum('iha,jha->hij', query_pos.astype(jnp.float32), key_pos.astype(jnp.float32))
    probs = lax.optimization_barrier((weights * scores).astype(jnp.bfloat16)).astype(jnp.float32)
    key_scale = jnp.exp(block_end[:, None] - cumulative).T
    decayed = lax.optimization_barrier((key_scale[:, :, None] * key_pos).astype(jnp.bfloat16)).astype(jnp.float32)
    end_scale = jnp.exp(stretch_end).T
    return (query_pos, key_pos, weights, probs, key_scale, decayed, end_scale, jnp.exp(block_end))

def reference(query_input, key_input, value_input, log_decay, stretch_ids, norm_gain, out_weight, out_cotangent):
    highest = lax.Precision.HIGHEST
    blocks = N_TM
    shape_four = (blocks, TOK_DEV, LOCAL_HEADS, HD)
    query_blocks = query_input.reshape(shape_four)
    key_blocks = key_input.reshape(shape_four)
    value_blocks = value_input.reshape(shape_four)
    decay_blocks = log_decay.reshape(LOCAL_HEADS, blocks, TOK_DEV).transpose(1, 0, 2)
    stretch_blocks = stretch_ids.reshape(blocks, TOK_DEV)

    def forward_step(prefix, inputs):
        query_blk, key_blk, value_blk, decay_blk, stretch_blk = inputs
        query_pos, key_pos, weights, probs, key_scale, decayed, end_scale, block_decay = local_parts(query_blk, key_blk, decay_blk, stretch_blk)
        value_wide = value_blk.astype(jnp.float32)
        local_out = jnp.einsum('hij,jhb->ihb', probs, value_wide)
        carried = jnp.einsum('iha,hab->ihb', query_pos.astype(jnp.float32), prefix, precision=highest)
        mixed = local_out + end_scale[:, :, None] * carried
        state = jnp.einsum('jha,jhb->hab', decayed, value_wide)
        return (block_decay[:, None, None] * prefix + state, (mixed, prefix))
    start_state = jnp.zeros((LOCAL_HEADS, HD, HD), jnp.float32)
    unused_state, (mixed_all, prefix_all) = lax.scan(forward_step, start_state, (query_blocks, key_blocks, value_blocks, decay_blocks, stretch_blocks))
    inv_rms = lax.rsqrt(lax.optimization_barrier(jnp.mean(mixed_all * mixed_all, axis=3)) + 1e-06)
    gain_heads = norm_gain.reshape(LOCAL_HEADS, HD)
    attended = (mixed_all * inv_rms[..., None] * gain_heads).astype(jnp.bfloat16).reshape(SEQUENCE_TOKENS, LOCAL_HEADS * HD)
    group_rows = LOCAL_HEADS // N_TENSOR * HD
    total = jnp.zeros((SEQUENCE_TOKENS, DOUT), jnp.float32)
    for member in range(N_TENSOR):
        partial_out = jnp.dot(attended[:, member * group_rows:(member + 1) * group_rows], out_weight[member * group_rows:(member + 1) * group_rows], preferred_element_type=jnp.float32).astype(jnp.bfloat16)
        total = total + lax.optimization_barrier(partial_out).astype(jnp.float32)
    layer_out = total.astype(jnp.bfloat16)
    out_grad = jnp.dot(out_cotangent, out_weight.T, preferred_element_type=jnp.float32).reshape(shape_four)
    gained = out_grad * gain_heads
    along = lax.optimization_barrier(jnp.mean(mixed_all * gained, axis=3))
    cube = inv_rms * inv_rms * inv_rms
    mixed_grad = (inv_rms[..., None] * gained - mixed_all * (cube * along)[..., None]).astype(jnp.bfloat16)

    def backward_step(later, inputs):
        query_blk, key_blk, value_blk, decay_blk, stretch_blk, grad_blk, prefix = inputs
        query_pos, key_pos, weights, probs, key_scale, decayed, end_scale, block_decay = local_parts(query_blk, key_blk, decay_blk, stretch_blk)
        value_wide = value_blk.astype(jnp.float32)
        grad_wide = lax.optimization_barrier(grad_blk).astype(jnp.float32)
        prob_grad = jnp.einsum('ihb,jhb->hij', grad_wide, value_wide)
        score_grad = lax.optimization_barrier((weights * prob_grad).astype(jnp.bfloat16)).astype(jnp.float32)
        value_local = jnp.einsum('hij,ihb->jhb', probs, grad_wide)
        query_local = jnp.einsum('hij,jha->iha', score_grad, key_pos.astype(jnp.float32))
        key_local = jnp.einsum('hij,iha->jha', score_grad, query_pos.astype(jnp.float32))
        scaled_query = lax.optimization_barrier((end_scale[:, :, None] * query_pos).astype(jnp.bfloat16)).astype(jnp.float32)
        state_grad = jnp.einsum('iha,ihb->hab', scaled_query, grad_wide)
        value_carry = jnp.einsum('jha,hab->jhb', decayed, later, precision=highest)
        key_carry = key_scale[:, :, None] * jnp.einsum('jhb,hab->jha', value_wide, later, precision=highest)
        query_carry = end_scale[:, :, None] * jnp.einsum('ihb,hab->iha', grad_wide, prefix, precision=highest)
        query_grad = jnp.where(query_blk > 0, query_local + query_carry, 0.0).astype(jnp.bfloat16)
        key_grad = jnp.where(key_blk > 0, key_local + key_carry, 0.0).astype(jnp.bfloat16)
        value_grad = (value_local + value_carry).astype(jnp.bfloat16)
        return (state_grad + block_decay[:, None, None] * later, (query_grad, key_grad, value_grad))
    unused_grad, (query_grad, key_grad, value_grad) = lax.scan(backward_step, start_state, (query_blocks, key_blocks, value_blocks, decay_blocks, stretch_blocks, mixed_grad, prefix_all), reverse=True)
    flat = (SEQUENCE_TOKENS, LOCAL_HEADS * HD)
    return (layer_out, query_grad.reshape(flat), key_grad.reshape(flat), value_grad.reshape(flat))
```

```python
import jax
import jax.numpy as jnp
from jax import lax
from jax.experimental import pallas as pl
from jax.experimental.pallas import tpu as pltpu
from jax.sharding import PartitionSpec as P

EPSILON = 1e-06


def forward_scan_kernel(got_ref, out_ref, gate_ref):
    count = got_ref.shape[0]
    rows = out_ref.shape[1]
    got = got_ref[...].astype(jnp.float32)
    decay = got[:, rows : rows + 1, :] + got[:, rows + 1 : rows + 2, :] + got[:, rows + 2 : rows + 3, :]
    gate = jnp.exp(decay)
    gate_ref[...] = jnp.broadcast_to(gate, gate_ref.shape)
    state = jnp.zeros(out_ref.shape[1:], jnp.float32)
    for block in range(count):
        out_ref[block] = state.astype(out_ref.dtype)
        state = gate[block] * state + got[block, :rows, :]


def reverse_scan_kernel(got_ref, gate_ref, out_ref):
    count = got_ref.shape[0]
    state = jnp.zeros(out_ref.shape[1:], jnp.float32)
    for block in range(count - 1, -1, -1):
        out_ref[block] = state.astype(out_ref.dtype)
        state = gate_ref[block] * state + got_ref[block].astype(jnp.float32)


def exchange(pieces):
    return lax.all_to_all(pieces, "tm", 0, 0, tiled=True)


def entering_forward(block_state, block_end, count):
    heads, size, width = block_state.shape
    rows = heads * size // count
    pieces = block_state.reshape(count, rows, width).astype(jnp.bfloat16)
    high = block_end.astype(jnp.bfloat16)
    rest = block_end - high.astype(jnp.float32)
    middle = rest.astype(jnp.bfloat16)
    low = (rest - middle.astype(jnp.float32)).astype(jnp.bfloat16)
    parts = jnp.stack([high, middle, low, jnp.zeros_like(low)], axis=1)
    parts = jnp.repeat(parts, count // heads, axis=0)
    tail = jnp.broadcast_to(parts[:, :, None], (count, 4, width))
    got = exchange(jnp.concatenate([pieces, tail], axis=1))
    mine, gate = pl.pallas_call(
        forward_scan_kernel,
        out_shape=(
            jax.ShapeDtypeStruct((count, rows, width), jnp.bfloat16),
            jax.ShapeDtypeStruct((count, rows, width), jnp.float32),
        ),
    )(got)
    return exchange(mine).reshape(heads, size, width), gate


def entering_reverse(state_grad, gate, count):
    heads, size, width = state_grad.shape
    rows = heads * size // count
    got = exchange(state_grad.reshape(count, rows, width).astype(jnp.bfloat16))
    mine = pl.pallas_call(
        reverse_scan_kernel,
        out_shape=jax.ShapeDtypeStruct((count, rows, width), jnp.bfloat16),
    )(got, gate)
    return exchange(mine).reshape(heads, size, width)


def on_device(
    query_input,
    key_input,
    value_input,
    log_decay,
    stretch_ids,
    norm_gain,
    out_weight,
    out_cotangent,
):
    tok_rows = query_input.shape[0]
    heads = log_decay.shape[0]
    head_size = query_input.shape[1] // heads
    query_pos = jnp.maximum(query_input, 0).reshape(tok_rows, heads, head_size)
    key_pos = jnp.maximum(key_input, 0).reshape(tok_rows, heads, head_size)
    value_act = value_input.reshape(tok_rows, heads, head_size)
    cumulative = jnp.cumsum(log_decay, axis=1)
    same_stretch = stretch_ids[:, None] == stretch_ids[None, :]
    visible = stretch_ids[None, :] <= stretch_ids[:, None]
    stretch_end = jnp.min(jnp.where(same_stretch[None], cumulative[:, None, :], jnp.inf), axis=2)
    block_end = cumulative[:, -1]
    weights = jnp.where(
        visible[None],
        jnp.exp(jnp.minimum(stretch_end[:, :, None] - cumulative[:, None, :], 0.0)),
        0.0,
    )
    scores = jnp.einsum("iha,jha->hij", query_pos, key_pos, preferred_element_type=jnp.float32)
    probs = (weights * scores).astype(jnp.bfloat16)
    local_out = jnp.einsum("hij,jhb->ihb", probs, value_act, preferred_element_type=jnp.float32)
    key_scale = jnp.exp(block_end[:, None] - cumulative).T
    decayed = (key_scale[:, :, None] * key_pos).astype(jnp.bfloat16)
    block_state = jnp.einsum("jha,jhb->hab", decayed, value_act, preferred_element_type=jnp.float32)
    prefix, gate = entering_forward(block_state, block_end, lax.axis_size("tm"))
    end_scale = jnp.exp(stretch_end).T
    carried = jnp.einsum("iha,hab->ihb", query_pos, prefix, preferred_element_type=jnp.float32)
    mixed = local_out + end_scale[:, :, None] * carried
    inv_rms = lax.rsqrt(jnp.mean(mixed * mixed, axis=2) + EPSILON)
    gain_heads = norm_gain.reshape(heads, head_size)
    attended = (
        (mixed * inv_rms[:, :, None] * gain_heads)
        .astype(jnp.bfloat16)
        .reshape(tok_rows, heads * head_size)
    )
    layer_out = lax.psum_scatter(
        jnp.dot(attended, out_weight, preferred_element_type=jnp.float32).astype(jnp.bfloat16),
        "tensor",
        scatter_dimension=0,
        tiled=True,
    )
    out_grad = lax.dot_general(
        lax.all_gather(out_cotangent, "tensor", axis=0, tiled=True),
        out_weight,
        (((1,), (1,)), ((), ())),
        preferred_element_type=jnp.float32,
    ).reshape(tok_rows, heads, head_size)
    gained = out_grad * gain_heads
    along = jnp.mean(mixed * gained, axis=2)
    cube = inv_rms * inv_rms * inv_rms
    mixed_grad = (inv_rms[:, :, None] * gained - mixed * (cube * along)[:, :, None]).astype(
        jnp.bfloat16
    )
    prob_grad = jnp.einsum(
        "ihb,jhb->hij", mixed_grad, value_act, preferred_element_type=jnp.float32
    )
    score_grad = (weights * prob_grad).astype(jnp.bfloat16)
    value_local = jnp.einsum("hij,ihb->jhb", probs, mixed_grad, preferred_element_type=jnp.float32)
    query_local = jnp.einsum(
        "hij,jha->iha", score_grad, key_pos, preferred_element_type=jnp.float32
    )
    key_local = jnp.einsum(
        "hij,iha->jha", score_grad, query_pos, preferred_element_type=jnp.float32
    )
    scaled_query = (end_scale[:, :, None] * query_pos).astype(jnp.bfloat16)
    state_grad = jnp.einsum(
        "iha,ihb->hab", scaled_query, mixed_grad, preferred_element_type=jnp.float32
    )
    later = entering_reverse(state_grad, gate, lax.axis_size("tm"))
    value_carry = jnp.einsum("jha,hab->jhb", decayed, later, preferred_element_type=jnp.float32)
    key_carry = key_scale[:, :, None] * jnp.einsum(
        "jhb,hab->jha", value_act, later, preferred_element_type=jnp.float32
    )
    query_carry = end_scale[:, :, None] * jnp.einsum(
        "ihb,hab->iha", mixed_grad, prefix, preferred_element_type=jnp.float32
    )
    flat = (tok_rows, heads * head_size)
    query_grad = (
        jnp.where(
            query_input.reshape(tok_rows, heads, head_size) > 0, query_local + query_carry, 0.0
        )
        .astype(jnp.bfloat16)
        .reshape(flat)
    )
    key_grad = (
        jnp.where(key_input.reshape(tok_rows, heads, head_size) > 0, key_local + key_carry, 0.0)
        .astype(jnp.bfloat16)
        .reshape(flat)
    )
    value_grad = (value_local + value_carry).astype(jnp.bfloat16).reshape(flat)
    return (layer_out, query_grad, key_grad, value_grad)


def solution(mesh):
    return jax.shard_map(
        on_device,
        mesh=mesh,
        in_specs=(
            P("tm", "tensor"),
            P("tm", "tensor"),
            P("tm", "tensor"),
            P("tensor", "tm"),
            P("tm"),
            P("tensor"),
            P("tensor", None),
            P(("tm", "tensor"), None),
        ),
        out_specs=(
            P(("tm", "tensor"), None),
            P("tm", "tensor"),
            P("tm", "tensor"),
            P("tm", "tensor"),
        ),
        check_vma=False,
    )
```
